256 devices in a mesh: seq: 32 (over z, y), head: 8 (over x, core).
Axes of the slice: x: 4, y: 4, z: 8, core: 2. Of those that a mesh axis runs over, the one named last changes fastest.
Arguments:
- query_in: bfloat16 [32768, 32, 128], P(('seq', 'head')), may hold values from -6 to 6
- key_in: bfloat16 [32768, 32, 128], P(('seq', 'head')), may hold values from -6 to 6
- value_in: bfloat16 [32768, 32, 128], P(('seq', 'head')), may hold values from -6 to 6
- grad_out: bfloat16 [32768, 32, 128], P(('seq', 'head')), may hold values from -6 to 6
- log_decay: bfloat16 [32768, 32], P(('seq', 'head')), may hold values from -1 to 0, as said below
Outputs:
- attended: bfloat16 [32768, 32, 128], P(('seq', 'head'))
- grad_query: bfloat16 [32768, 32, 128], P(('seq', 'head'))
- grad_key: bfloat16 [32768, 32, 128], P(('seq', 'head'))
- grad_value: bfloat16 [32768, 32, 128], P(('seq', 'head'))
The draws below stay inside these ranges and needn't reach their ends.
Inputs may be any that keep to these rules, and one draw needn't show every extreme that they name: Every entry of log_decay is negative.
All inputs are finite; a program needn't handle non-finite values.
Results may differ from the reference program's by a relative error of at most 0.007.
Values may be sent and summed in bfloat16 or wider, within the bound.
A program may use at most 128 MiB of HBM per device.

```python
import math
import jax
import jax.numpy as jnp
from jax import lax

HEADS = 32
DH = 128
SEG = 1024
TOKENS = 32768
N_SEQ = 32


def draw_log_decay(key, part):
    parallel_flows = jax.random.split(key, 6)
    share = 0.5
    slowish = jax.random.uniform(parallel_flows[0], (HEADS,)) < share
    slow_rate = jnp.exp(jax.random.uniform(parallel_flows[1], (HEADS,), minval=math.log(0.05), maxval=math.log(0.4))) / TOKENS
    fast_rate = jnp.exp(jax.random.uniform(parallel_flows[2], (HEADS,), minval=math.log(1.0 / 50.0), maxval=math.log(1.0 / 30.0)))
    base_rate = jnp.where(slowish, slow_rate, fast_rate)
    blocks = TOKENS // SEG
    factor = jnp.exp(jax.random.uniform(parallel_flows[3], (blocks, 1, HEADS), minval=-math.log(2.0), maxval=math.log(2.0)))
    forgetting_factors = jnp.broadcast_to(base_rate[None, None, :] * factor, (blocks, SEG, HEADS)).reshape(TOKENS, HEADS)
    piece_locations = jax.random.randint(parallel_flows[4], (2, HEADS), 0, TOKENS)
    shrink_factor = jax.random.uniform(parallel_flows[5], (2, HEADS), minval=0.2, maxval=0.5)
    element_index_within = jnp.arange(TOKENS)[:, None, None]
    contiguous_ranges = jnp.sum(jnp.where(element_index_within == piece_locations[None, :, :], -jnp.log1p(-shrink_factor)[None, :, :], 0.0), axis=1)
    return (-forgetting_factors - contiguous_ranges).astype(jnp.float32).astype(jnp.bfloat16)


def block_levels(key, extent, cuts, smallest, top_value):
    gain, own = 1.0, jax.random.fold_in(key, 6)
    for axis_at, blocks in cuts:
        steps = jnp.exp(jax.random.uniform(jax.random.fold_in(own, axis_at), (blocks,), jnp.float32, smallest / len(cuts), top_value / len(cuts)))
        gain = gain * jnp.repeat(steps, extent[axis_at] // blocks).reshape([-1 if axis == axis_at else 1 for axis in range(len(extent))])
    return gain


def normal_values(stream_key, dims, width, bound, cuts=(), held_as=jnp.bfloat16):
    entries = width * jax.random.normal(stream_key, dims, jnp.float32)
    if cuts:
        entries = entries * block_levels(stream_key, dims, cuts, -0.22, 0.18)
    return jnp.clip(entries, -bound, bound).astype(held_as)


def setup_inputs(seed: int = 0) -> dict:
    seeds = jax.random.split(jax.random.key(seed), 6)
    return {
        "query_in": normal_values(seeds[0], (TOKENS, HEADS, DH), 1.0, 6.0, ((0, 256),)),
        "key_in": normal_values(seeds[1], (TOKENS, HEADS, DH), 1.0, 6.0, ((0, 256),)),
        "value_in": normal_values(seeds[2], (TOKENS, HEADS, DH), 1.0, 6.0, ((0, 256),)),
        "grad_out": normal_values(seeds[3], (TOKENS, HEADS, DH), 1.0, 6.0, ((0, 256),)),
        "log_decay": draw_log_decay(jax.random.fold_in(seeds[5], 71), 0),
    }


precise = lax.Precision.HIGHEST


def rounded(array):
    return lax.optimization_barrier(array.astype(jnp.bfloat16)).astype(jnp.float32)


def single_attention_unit(operands):
    queries, keys_all, values, grads, token_decays = operands
    f32 = jnp.float32
    scaling = 1.0 / DH
    queries = queries.astype(f32)
    keys_all = keys_all.astype(f32)
    values = values.astype(f32)
    grads = grads.astype(f32)
    within = jnp.cumsum(token_decays.astype(f32), axis=1)
    seg_total = within[:, -1]
    to_start = jnp.exp(within)[:, :, None]
    to_end = jnp.exp(seg_total[:, None] - within)[:, :, None]
    causal = jnp.arange(SEG)[:, None] >= jnp.arange(SEG)[None, :]
    gap_log = within[:, :, None] - within[:, None, :]
    decay_mat = jnp.where(causal, jnp.exp(jnp.where(causal, gap_log, 0.0)), 0.0)
    scores = jnp.einsum('ntd,nsd->nts', queries, keys_all, precision=precise)
    attn_w = rounded(scaling * scores * decay_mat)
    intra = jnp.einsum('nts,nsd->ntd', attn_w, values, precision=precise)
    keys_end = rounded(keys_all * to_end)
    values_end = rounded(values * to_end)
    queries_start = rounded(queries * to_start)
    grads_start = rounded(grads * to_start)
    local_kv = rounded(jnp.einsum('ntd,nte->nde', keys_end, values, precision=precise))
    local_qg = rounded(jnp.einsum('ntd,nte->nde', queries_start, grads, precision=precise))
    cum_inc = jnp.cumsum(seg_total)
    cum_exc = cum_inc - seg_total
    ranks = jnp.arange(N_SEQ)
    earlier = ranks[None, :] < ranks[:, None]
    later_on = ranks[None, :] > ranks[:, None]
    w_in = jnp.where(earlier, jnp.exp(jnp.where(earlier, cum_exc[:, None] - cum_inc[None, :], 0.0)), 0.0)
    w_out = jnp.where(later_on, jnp.exp(jnp.where(later_on, cum_exc[None, :] - cum_inc[:, None], 0.0)), 0.0)
    state_in = rounded(jnp.einsum('ji,ide->jde', w_in, local_kv, precision=precise))
    state_out = rounded(jnp.einsum('ji,ide->jde', w_out, local_qg, precision=precise))
    attended = (intra + scaling * jnp.einsum('ntd,nde->nte', queries_start, state_in, precision=precise)).astype(jnp.bfloat16)
    back_raw = jnp.einsum('nte,nse->nts', grads, values, precision=precise)
    back_w = rounded(scaling * back_raw * decay_mat)
    grad_query = (jnp.einsum('nts,nsd->ntd', back_w, keys_all, precision=precise)
                  + scaling * jnp.einsum('nte,nde->ntd', grads_start, state_in, precision=precise)).astype(jnp.bfloat16)
    grad_key = (jnp.einsum('nts,ntd->nsd', back_w, queries, precision=precise)
                + scaling * jnp.einsum('nse,nde->nsd', values_end, state_out, precision=precise)).astype(jnp.bfloat16)
    grad_value = (jnp.einsum('nts,nte->nse', attn_w, grads, precision=precise)
                  + scaling * jnp.einsum('nsd,nde->nse', keys_end, state_out, precision=precise)).astype(jnp.bfloat16)
    return attended, grad_query, grad_key, grad_value


def head_major(array):
    return array.reshape(N_SEQ, SEG, HEADS, DH).transpose(2, 0, 1, 3)


def reference(query_in, key_in, value_in, grad_out, log_decay):
    token_decays = log_decay.reshape(N_SEQ, SEG, HEADS).transpose(2, 0, 1)
    results = lax.map(single_attention_unit, (head_major(query_in), head_major(key_in), head_major(value_in), head_major(grad_out), token_decays))
    return tuple(item.transpose(1, 2, 0, 3).reshape(TOKENS, HEADS, DH) for item in results)
```

```python
import functools

import jax
import jax.numpy as jnp
from jax import lax
from jax.experimental import pallas as pl
from jax.experimental.pallas import tpu as pltpu
from jax.sharding import PartitionSpec as P

MESH = pl.DeviceIdType.MESH
bf16 = jnp.bfloat16
f32 = jnp.float32
NN = (((1,), (0,)), ((), ()))
NT = (((1,), (1,)), ((), ()))
TN = (((0,), (0,)), ((), ()))
PAIRS, NX, NB, NS, ROWS = 16, 4, 2, 32, 16


def dot(a, b, dims=NN):
    return lax.dot_general(a, b, dims, preferred_element_type=f32)


def drain(ref, sem):
    pltpu.make_async_copy(ref, ref, sem).wait()


def kernel(
    l_ref, q_hbm, k_hbm, v_hbm, g_hbm, o_att, o_gq, o_gk, o_gv,
    inb, outb, acc, es_t, ee_t, lf, upper, mask, s_own, s_send, s_recv, c_buf, x_recv, y_send, y_recv,
    z_send, w_recv, d_buf, in_buf, p_send, fin, t_core, t_x, t_y, w_tab, x_tab, f_tab,
    in_sem, out_sem, tc_s, tc_r, tx_s, tx_r, ty_s, ty_r, cu_s, cu_r, xu_s, xu_r, yu_s, yu_r,
    yd_s, yd_r, xd_s, xd_r, cd_s, cd_r,
):
    seg = lax.axis_index("seq")
    head = lax.axis_index("head")
    chip, core = head // 2, head % 2
    other = 1 - core
    partner = {"head": chip * 2 + other}
    scaling = 1.0 / 128
    sources = (q_hbm, k_hbm, v_hbm, g_hbm)
    targets = (o_att, o_gq, o_gk, o_gv)

    def ring(d):
        return lax.rem(chip + d, NX)

    barrier = pltpu.get_barrier_semaphore()
    pl.semaphore_signal(barrier, inc=1, device_id=partner, device_id_type=MESH)
    for d in range(1, NX):
        pl.semaphore_signal(barrier, inc=1, device_id={"head": ring(d) * 2 + core}, device_id_type=MESH)

    def greet(i, _):
        pl.semaphore_signal(barrier, inc=1, device_id={"seq": lax.rem(seg + i, NS)}, device_id_type=MESH)
        return 0

    lax.fori_loop(1, NS, greet, 0)

    def load(n, _):
        side = (n // 4) % 2
        half = other + side * (core - other)
        pair = half * 8 + (n // 8) * 4 + n % 4
        for a in range(4):
            pltpu.make_async_copy(sources[a].at[:, pair], inb.at[pair, a], in_sem.at[pair]).start()
        return 0

    lax.fori_loop(0, PAIRS, load, 0)

    logs = l_ref[...]
    lf[...] = logs.astype(f32)
    padded = jnp.concatenate([logs, jnp.zeros((96, 128), bf16)], axis=0)
    t_core[core] = dot(jnp.ones((8, 128), bf16), padded, NT)
    row2 = lax.broadcasted_iota(jnp.int32, (256, 256), 0)
    col2 = lax.broadcasted_iota(jnp.int32, (256, 256), 1)
    mask[...] = jnp.where((row2 % 2 == col2 % 2) & (row2 >= col2), scaling, 0.0)
    upper[...] = jnp.where(
        lax.broadcasted_iota(jnp.int32, (128, 256), 0) > lax.broadcasted_iota(jnp.int32, (128, 256), 1) // 2, 1.0, 0.0
    ).astype(bf16)
    row = lax.broadcasted_iota(jnp.int32, (256, 128), 0)
    lane = lax.broadcasted_iota(jnp.int32, (256, 128), 1)
    odd = row % 2 == 1
    upto = lane <= row // 2
    ones = jnp.ones((128, 128), bf16)

    def log_rows(pair):
        return jnp.where(odd, lf[pl.ds(2 * pair + 1, 1), :], lf[pl.ds(2 * pair, 1), :])

    def per_head(line):
        r = lax.broadcasted_iota(jnp.int32, (32, 128), 0)
        c = lax.broadcasted_iota(jnp.int32, (32, 128), 1)
        total = jnp.sum(jnp.where(r == c, line, 0.0), axis=1, keepdims=True)
        return jnp.broadcast_to(jnp.exp(total), (32, 128))

    def inputs(pair):
        return [inb.at[pair, a].reshape(256, 128)[...] for a in range(4)]

    def local_state(pair):
        drain(inb.at[pair], in_sem.at[pair])
        q, k, v, g = inputs(pair)
        whole = log_rows(pair)
        es = jnp.exp(dot(jnp.where(upto, whole, 0.0).astype(bf16), ones))
        ee = jnp.exp(dot(jnp.where(upto, 0.0, whole).astype(bf16), ones))
        es_t[pair] = es
        ee_t[pair] = ee

        def split(x):
            return jnp.concatenate([jnp.where(odd, 0.0, x), jnp.where(odd, x, 0.0)], axis=1).astype(bf16)

        return dot(k, split(v.astype(f32) * ee), TN), dot(q, split(g.astype(f32) * es), TN)

    def states(b):
        def theirs(i, _):
            for kind, s in enumerate(local_state(other * 8 + b * 4 + i)):
                s_send[b, i, kind, 0:128, :] = s[:, 0:128].astype(bf16)
                s_send[b, i, kind, 128:256, :] = s[:, 128:256].astype(bf16)
            return 0

        lax.fori_loop(0, 4, theirs, 0)
        up = pltpu.make_async_remote_copy(
            s_send.at[b], s_recv.at[b], cu_s.at[b], cu_r.at[b], device_id=partner, device_id_type=MESH
        )
        up.start()

        def mine(i, _):
            for kind, s in enumerate(local_state(core * 8 + b * 4 + i)):
                s_own[b, i, kind, 0:128, :] = s[:, 0:128]
                s_own[b, i, kind, 128:256, :] = s[:, 128:256]
            return 0

        lax.fori_loop(0, 4, mine, 0)

    def chip_states(b):
        drain(s_recv.at[b], cu_r.at[b])

        def one(i, _):
            for kind in range(2):
                for hd in range(2):
                    at = pl.ds(2 * (core * 8 + b * 4 + i) + hd, 1)
                    r = pl.ds(hd * 128, 128)
                    c_buf[b, i, kind, r, :] = (
                        w_tab[2 * kind, at, :] * s_own[b, i, kind, r, :]
                        + w_tab[2 * kind + 1, at, :] * s_recv[b, i, kind, r, :].astype(f32)
                    ).astype(bf16)
            return 0

        lax.fori_loop(0, 4, one, 0)
        for d in range(1, NX):
            pltpu.make_async_remote_copy(
                c_buf.at[b, ring(d)], x_recv.at[b, chip], xu_s.at[b], xu_r.at[b],
                device_id={"head": ring(d) * 2 + core}, device_id_type=MESH,
            ).start()
        x_recv[b, chip] = c_buf[b, chip]

    def seg_states(b):
        drain(x_recv.at[b, pl.ds(0, 3)], xu_r.at[b])
        pair = core * 8 + b * 4 + chip
        for hd in range(2):
            at = pl.ds(2 * pair + hd, 1)
            r = pl.ds(hd * 128, 128)
            kv = x_recv[b, 0, 0, r, :].astype(f32)
            qg = x_recv[b, 3, 1, r, :].astype(f32)
            for i in range(1, NX):
                kv = kv * x_tab[i, at, :] + x_recv[b, i, 0, r, :].astype(f32)
                qg = qg * x_tab[3 - i, at, :] + x_recv[b, 3 - i, 1, r, :].astype(f32)
            y_send[b, r, :] = kv.astype(bf16)
            y_send[b, pl.ds(256 + hd * 128, 128), :] = qg.astype(bf16)

        def send(i, _):
            to = lax.rem(seg + i, NS)
            pltpu.make_async_remote_copy(
                y_send.at[b, pl.ds(pl.multiple_of(to * ROWS, ROWS), ROWS)], y_recv.at[b, seg], yu_s.at[b], yu_r.at[b],
                device_id={"seq": to}, device_id_type=MESH,
            ).start()
            return 0

        lax.fori_loop(1, NS, send, 0)
        y_recv[b, seg] = y_send[b, pl.ds(pl.multiple_of(seg * ROWS, ROWS), ROWS), :]

    def scan_segments(b):
        drain(y_recv.at[b, pl.ds(0, NS - 1)], yu_r.at[b])
        back = seg // 16

        def step(i, total):
            j = i + back * (31 - 2 * i)
            z_send[b, j] = total.astype(bf16)
            return total * f_tab[b, pl.ds(j, 1), :] + y_recv[b, j].astype(f32)

        lax.fori_loop(0, NS, step, jnp.zeros((ROWS, 128), f32), unroll=4)

        def send(i, _):
            to = lax.rem(seg + i, NS)
            pltpu.make_async_remote_copy(
                z_send.at[b, to], w_recv.at[b, pl.ds(pl.multiple_of(seg * ROWS, ROWS), ROWS)], yd_s.at[b], yd_r.at[b],
                device_id={"seq": to}, device_id_type=MESH,
            ).start()
            return 0

        lax.fori_loop(1, NS, send, 0)
        w_recv[b, pl.ds(pl.multiple_of(seg * ROWS, ROWS), ROWS), :] = z_send[b, seg]

    def chip_entries(b):
        drain(w_recv.at[b, pl.ds(0, (NS - 1) * ROWS)], yd_r.at[b])
        pair = core * 8 + b * 4 + chip
        for hd in range(2):
            at = pl.ds(2 * pair + hd, 1)
            r = pl.ds(hd * 128, 128)
            kv = w_recv[b, r, :].astype(f32)
            qg = w_recv[b, pl.ds(256 + hd * 128, 128), :].astype(f32)
            for i in range(NX):
                d_buf[b, i, 0, r, :] = kv.astype(bf16)
                d_buf[b, 3 - i, 1, r, :] = qg.astype(bf16)
                if i < NX - 1:
                    kv = kv * x_tab[i, at, :] + x_recv[b, i, 0, r, :].astype(f32)
                    qg = qg * x_tab[3 - i, at, :] + x_recv[b, 3 - i, 1, r, :].astype(f32)
        for d in range(1, NX):
            pltpu.make_async_remote_copy(
                d_buf.at[b, ring(d)], in_buf.at[b, chip], xd_s.at[b], xd_r.at[b],
                device_id={"head": ring(d) * 2 + core}, device_id_type=MESH,
            ).start()
        in_buf[b, chip] = d_buf[b, chip]

    def core_entries(b):
        drain(in_buf.at[b, pl.ds(0, 3)], xd_r.at[b])
        first = (1 - core).astype(f32)
        second = core.astype(f32)

        def one(i, _):
            for kind in range(2):
                for hd in range(2):
                    at = pl.ds(2 * (core * 8 + b * 4 + i) + hd, 1)
                    r = pl.ds(hd * 128, 128)
                    entry = in_buf[b, i, kind, r, :].astype(f32)
                    use_mine, use_theirs = (second, first) if kind == 0 else (first, second)
                    tab = 2 - 2 * kind
                    fin[core, b, i, kind, r, :] = (
                        entry * w_tab[tab, at, :] + use_mine * s_recv[b, i, kind, r, :].astype(f32)
                    ).astype(bf16)
                    p_send[b, i, kind, r, :] = (
                        entry * w_tab[tab + 1, at, :] + use_theirs * s_own[b, i, kind, r, :]
                    ).astype(bf16)
            return 0

        lax.fori_loop(0, 4, one, 0)
        pltpu.make_async_remote_copy(
            p_send.at[b], fin.at[core, b], cd_s.at[b], cd_r.at[b], device_id=partner, device_id_type=MESH
        ).start()

    def intra(pair, _):
        q, k, v, g = inputs(pair)
        logs_to = jnp.where(upto, log_rows(pair), 0.0).astype(bf16)
        decay = jnp.exp(dot(logs_to, upper[...])) * mask[...]
        attn = (dot(q, k, NT) * decay).astype(bf16)
        back = (dot(g, v, NT) * decay).astype(bf16)
        acc[pair, 0] = dot(attn, v)
        acc[pair, 1] = dot(back, k)
        acc[pair, 2] = dot(back, q, TN)
        acc[pair, 3] = dot(attn, g, TN)
        return 0

    def finish(half, b):
        def one(i, _):
            pair = half * 8 + b * 4 + i
            q, k, v, g = inputs(pair)
            es = es_t[pair] * scaling
            ee = ee_t[pair] * scaling
            si = fin[half, b, i, 0]
            so = fin[half, b, i, 1]

            def pick(x):
                return jnp.where(odd, x[:, 128:256], x[:, 0:128])

            def put(a, scale, x):
                outb.at[pair, a].reshape(256, 128)[...] = (acc[pair, a] + scale * x).astype(bf16)
                pltpu.make_async_copy(outb.at[pair, a], targets[a].at[:, pair], out_sem.at[pair]).start()

            put(0, es, jnp.where(odd, dot(q, si[128:256]), dot(q, si[0:128])))
            put(1, es, pick(dot(g, si, NT)))
            put(2, ee, pick(dot(v, so, NT)))
            put(3, ee, jnp.where(odd, dot(k, so[128:256]), dot(k, so[0:128])))
            return 0

        lax.fori_loop(0, 4, one, 0)

    pl.semaphore_wait(barrier, NX + NS - 1)
    pltpu.make_async_remote_copy(
        t_core.at[core], t_core.at[core], tc_s, tc_r, device_id=partner, device_id_type=MESH
    ).start()

    states(0)
    drain(t_core.at[0], tc_r)
    t0, t1 = t_core[0], t_core[1]
    e0, e1 = per_head(t0[0:1]), per_head(t1[0:1])
    one_tab = jnp.ones_like(e0)
    w_tab[0] = jnp.where(core == 0, e1, one_tab)
    w_tab[1] = jnp.where(core == 0, one_tab, e1)
    w_tab[2] = jnp.where(core == 0, one_tab, e0)
    w_tab[3] = jnp.where(core == 0, e0, one_tab)
    t_x[chip] = t0 + t1
    for d in range(1, NX):
        pltpu.make_async_remote_copy(
            t_x.at[chip], t_x.at[chip], tx_s, tx_r, device_id={"head": ring(d) * 2 + core}, device_id_type=MESH
        ).start()
    chip_states(0)
    states(1)
    drain(t_x.at[pl.ds(0, 3)], tx_r)
    for i in range(NX):
        x_tab[i] = per_head(t_x[i, 0:1, :])
    t_y[seg] = t_x[0] + t_x[1] + t_x[2] + t_x[3]

    def tell(i, _):
        pltpu.make_async_remote_copy(
            t_y.at[seg], t_y.at[seg], ty_s, ty_r, device_id={"seq": lax.rem(seg + i, NS)}, device_id_type=MESH
        ).start()
        return 0

    lax.fori_loop(1, NS, tell, 0)
    chip_states(1)
    lax.fori_loop(0, 8, intra, 0)
    seg_states(0)
    drain(t_y.at[pl.ds(0, NS - 1)], ty_r)
    seg_logs = t_y[:, 0, :]
    for b in range(NB):
        mine = 2 * (core * 8 + b * 4 + chip) + (seg % 16) // 8
        lanes = lax.broadcasted_iota(jnp.int32, (NS, 128), 1)
        total = jnp.sum(jnp.where(lanes == mine, seg_logs, 0.0), axis=1, keepdims=True)
        f_tab[b] = jnp.broadcast_to(jnp.exp(total), (NS, 128))
    seg_states(1)
    scan_segments(0)
    lax.fori_loop(8, 16, intra, 0)
    scan_segments(1)
    for b in range(NB):
        chip_entries(b)
    for b in range(NB):
        core_entries(b)
        finish(core, b)
        drain(fin.at[other, b], cd_r.at[b])
        finish(other, b)

    drain(t_core.at[0], tc_s)
    drain(t_x.at[pl.ds(0, 3)], tx_s)
    drain(t_y.at[pl.ds(0, NS - 1)], ty_s)
    for b in range(NB):
        drain(s_send.at[b], cu_s.at[b])
        drain(c_buf.at[b, pl.ds(0, 3)], xu_s.at[b])
        drain(y_recv.at[b, pl.ds(0, NS - 1)], yu_s.at[b])
        drain(z_send.at[b, pl.ds(0, NS - 1)], yd_s.at[b])
        drain(d_buf.at[b, pl.ds(0, 3)], xd_s.at[b])
        drain(p_send.at[b], cd_s.at[b])

    def written(pair, _):
        drain(outb.at[pair], out_sem.at[pair])
        return 0

    lax.fori_loop(0, PAIRS, written, 0)


def shards(query_in, key_in, value_in, grad_out, log_decay):
    def paired(x):
        return x.reshape(128, PAIRS, 2, 128)

    vm, dma = pltpu.VMEM, pltpu.SemaphoreType.DMA
    five = (NB, 4, 2, 256, 128)
    scratch = [
        vm((PAIRS, 4, 128, 2, 128), bf16), vm((PAIRS, 4, 128, 2, 128), bf16), vm((PAIRS, 4, 256, 128), f32),
        vm((PAIRS, 256, 128), f32), vm((PAIRS, 256, 128), f32), vm((32, 128), f32), vm((128, 256), bf16),
        vm((256, 256), f32), vm(five, f32), vm(five, bf16), vm(five, bf16), vm(five, bf16), vm(five, bf16),
        vm((NB, 512, 128), bf16), vm((NB, NS, ROWS, 128), bf16), vm((NB, NS, ROWS, 128), bf16),
        vm((NB, 512, 128), bf16), vm(five, bf16), vm(five, bf16), vm(five, bf16), vm((2,) + five, bf16),
        vm((2, 8, 128), f32), vm((NX, 8, 128), f32), vm((NS, 8, 128), f32),
        vm((4, 32, 128), f32), vm((NX, 32, 128), f32), vm((NB, NS, 128), f32),
        dma((PAIRS,)), dma((PAIRS,)), dma, dma, dma, dma, dma, dma,
    ] + [dma((NB,))] * 12
    outs = pl.pallas_call(
        kernel,
        out_shape=[jax.ShapeDtypeStruct((128, PAIRS, 2, 128), bf16)] * 4,
        in_specs=[pl.BlockSpec(memory_space=pltpu.VMEM)] + [pl.BlockSpec(memory_space=pl.ANY)] * 4,
        out_specs=[pl.BlockSpec(memory_space=pl.ANY)] * 4,
        scratch_shapes=scratch,
        compiler_params=pltpu.CompilerParams(collective_id=0, has_side_effects=True, vmem_limit_bytes=60 << 20),
    )(log_decay.T, paired(query_in), paired(key_in), paired(value_in), paired(grad_out))
    return tuple(x.reshape(128, 32, 128) for x in outs)


def solution(mesh):
    spec = P(("seq", "head"), None, None)
    return jax.shard_map(
        shards,
        mesh=mesh,
        in_specs=(spec,) * 4 + (P(("seq", "head"), None),),
        out_specs=(spec,) * 4,
        check_vma=False,
    )
```
